32 devices in a mesh: group: 2 (over y), mid: 4 (over z), freq: 2 (over x), off: 2 (over core).
Axes of the slice: x: 2, y: 2, z: 4, core: 2. Of those that a mesh axis runs over, the one named last changes fastest.
Arguments:
- traces: bfloat16 [2, 1024, 1024], P('off', ('group', 'mid', 'freq')), parts along dimension 1, may hold values from -6 to 6
- time_filter: bfloat16 [1024, 1024], replicated, may hold values from -0.1875 to 0.1875
- midpoint_of: int32 [2, 1024], P('off', 'group'), parts along dimension 1, may hold values from 0 to 7, as said below
- offset_of: int32 [2, 1024], P('off', 'group'), parts along dimension 1, may hold values from 0 to 127, as said below
- shrink_level: float32 [512], P('freq'), may hold values from 0.2 to 2
Outputs:
- primaries: bfloat16 [2, 1024, 1024], P('off', ('group', 'mid', 'freq')), parts along dimension 1
The draws below stay inside these ranges and needn't reach their ends.
There are 2 independent parts, one for each index of `group`. The reference program is written for one: setup_inputs(seed, part) draws one part's arguments, and reference() takes and returns one part's arrays. A program takes and returns all parts, laid end to end along the dimension named above; an argument that names none is the same for every part. Nothing has to cross between parts.
Inputs may be any that keep to these rules, and one draw needn't show every extreme that they name: `midpoint_of`: together with offset_of, every (midpoint, offset) pair occurs exactly once in a part; the traces of one device (a block of 64 along the second dimension) go to midpoint owners (midpoint // 2) in counts of 32 for a quarter of the owners, 16 for another quarter and 8 for the rest, so at most 32 traces from one device reach one owner. `offset_of`: traces at first index o have offsets in o * 64 up to (o + 1) * 64 - 1.
All inputs are finite; a program needn't handle non-finite values.
Results may differ from the reference program's by a relative error of at most 0.0076.
Values may be sent and summed in bfloat16 or wider, within the bound.
A program may use at most 64 MiB of HBM per device.

```python
import math
import jax
import jax.numpy as jnp

NT = 1024
NF = 512
NOFF = 128
NP = 128
TR_DEV = 64
NCMP = 8
TRH = 512
N_MID = 4
N_FREQ = 2
N_OFF = 2


def geometry(key):
    base_key = jax.random.fold_in(key, 11)
    quota_rows = TR_DEV // N_MID
    noff_dev = NOFF // N_OFF
    cmp_dev = N_FREQ * TR_DEV // noff_dev
    owners = jnp.arange(N_MID, dtype=jnp.int32)
    profile = jnp.where(owners < N_MID // 4, 2 * quota_rows, jnp.where(owners < N_MID // 2, quota_rows, quota_rows // 2))
    bounds = jnp.cumsum(profile)
    places = jnp.arange(TR_DEV, dtype=jnp.int32)
    step_of = jnp.sum((places[:, None] >= bounds[None, :]).astype(jnp.int32), axis=1)
    senders = jnp.arange(N_MID * N_FREQ, dtype=jnp.int32)
    sender_mid = senders // N_FREQ
    sender_freq = senders % N_FREQ
    mid_rows = []
    off_rows = []
    for half_index in range(N_OFF):
        half_key = jax.random.fold_in(base_key, half_index)
        shifts = jax.random.randint(jax.random.fold_in(half_key, 1), (N_FREQ,), 0, N_MID)
        order_keys = jax.random.split(jax.random.fold_in(half_key, 2), N_MID * N_FREQ)
        orders = jax.vmap(lambda sub_key: jax.random.permutation(sub_key, TR_DEV))(order_keys)
        destination = (sender_mid[:, None] + shifts[sender_freq][:, None] + step_of[orders]) % N_MID
        flat_dest = destination.reshape(-1)
        onehot = (flat_dest[:, None] == owners[None, :]).astype(jnp.int32)
        rank_in = jnp.sum(jnp.cumsum(onehot, axis=0) * onehot, axis=1) - 1
        cell_keys = jax.random.split(jax.random.fold_in(half_key, 3), N_MID)
        cell_perm = jax.vmap(lambda sub_key: jax.random.permutation(sub_key, cmp_dev * noff_dev))(cell_keys)
        cell_pick = cell_perm[flat_dest, rank_in].astype(jnp.int32)
        mid_rows.append((flat_dest * cmp_dev + cell_pick // noff_dev).astype(jnp.int32))
        off_rows.append((half_index * noff_dev + cell_pick % noff_dev).astype(jnp.int32))
    return (jnp.stack(mid_rows), jnp.stack(off_rows))


def draw_midpoint_of(key, part):
    return geometry(key)[0]


def draw_offset_of(key, part):
    return geometry(key)[1]


def block_levels(rng, extent, pieces, low, high):
    def one(axis_at, blocks):
        heights = jax.random.uniform(jax.random.fold_in(jax.random.fold_in(rng, 6), axis_at), (blocks,), jnp.float32, low / len(pieces), high / len(pieces))
        return jnp.repeat(jnp.exp(heights), extent[axis_at] // blocks).reshape((-1,) + (1,) * (len(extent) - axis_at - 1))

    factor_of = one(*pieces[0])
    for cut in pieces[1:]:
        factor_of = factor_of * one(*cut)
    return factor_of


def noise(rng, dims, width, limit, cuts=(), kind=jnp.bfloat16):
    gain = block_levels(rng, dims, cuts, -0.22, 0.18) if cuts else 1.0
    values = jax.random.normal(rng, dims, jnp.float32) * width * gain
    return jnp.minimum(jnp.maximum(values, -limit), limit).astype(kind)


def setup_inputs(seed: int = 0, part: int = 0) -> dict:
    keys = jax.random.split(jax.random.key(seed), 6)
    part_keys = jax.random.split(jax.random.fold_in(keys[5], part), 6)
    return {
        "traces": noise(part_keys[0], (N_OFF, TRH, NT), 1.0, 6.0, ((0, 2), (1, 8))),
        "time_filter": noise(keys[1], (NT, NT), NT ** -0.5, 0.1875),
        "midpoint_of": draw_midpoint_of(jax.random.fold_in(jax.random.fold_in(keys[5], part), 71), part),
        "offset_of": draw_offset_of(jax.random.fold_in(jax.random.fold_in(keys[5], part), 71), part),
        "shrink_level": jnp.clip(jnp.exp(math.log(2.0) - 2.3025851 * jax.random.uniform(keys[4], (NF,), jnp.float32) ** block_levels(keys[4], (NF,), ((0, 2),), -0.2, 0.2)), 0.2, 2.0),
    }


two_pi = 2.0 * math.pi
radon_period = 4096

def dft_tables():
    sample = jnp.arange(NT, dtype=jnp.int32)[:, None]
    freq_index = jnp.arange(NF, dtype=jnp.int32)[None, :]
    angle = two_pi * (sample * freq_index % NT).astype(jnp.float32) / NT
    scale_f = 1.0 / math.sqrt(NT)
    cosine = (jnp.cos(angle) * scale_f).astype(jnp.bfloat16)
    sine = (-jnp.sin(angle) * scale_f).astype(jnp.bfloat16)
    return (cosine, sine)

def radon_tables():
    freq_index = jnp.arange(NF, dtype=jnp.int32)[:, None, None]
    offset_index = jnp.arange(NOFF, dtype=jnp.int32)[None, :, None]
    slowness = jnp.arange(NP, dtype=jnp.int32)[None, None, :]
    turns = freq_index * slowness % radon_period * (offset_index * offset_index % radon_period) % radon_period
    angle = two_pi * turns.astype(jnp.float32) / radon_period
    scale_r = 1.0 / math.sqrt(NOFF)
    return ((jnp.cos(angle) * scale_r).astype(jnp.bfloat16), (jnp.sin(angle) * scale_r).astype(jnp.bfloat16))

def smooth_edges(grid):
    padded = jnp.pad(grid.astype(jnp.float32), ((1, 1), (0, 0), (0, 0)))
    return ((padded[:-2] + 2.0 * padded[1:-1] + padded[2:]) * 0.25).astype(jnp.bfloat16)

def reference(traces, time_filter, midpoint_of, offset_of, shrink_level):
    flat_traces = traces.reshape(-1, NT)
    filtered = jnp.dot(flat_traces, time_filter, preferred_element_type=jnp.float32).astype(jnp.bfloat16)
    cos_tab, sin_tab = dft_tables()
    spec_re = jnp.dot(filtered, cos_tab, preferred_element_type=jnp.float32).astype(jnp.bfloat16)
    spec_im = jnp.dot(filtered, sin_tab, preferred_element_type=jnp.float32).astype(jnp.bfloat16)
    mids = midpoint_of.reshape(-1)
    offs = offset_of.reshape(-1)
    gather_re = jnp.zeros((NCMP, NOFF, NF), spec_re.dtype).at[mids, offs].set(spec_re)
    gather_im = jnp.zeros((NCMP, NOFF, NF), spec_im.dtype).at[mids, offs].set(spec_im)
    smooth_re = smooth_edges(gather_re).astype(jnp.float32)
    smooth_im = smooth_edges(gather_im).astype(jnp.float32)
    rad_cos, rad_sin = radon_tables()
    rad_cos = rad_cos.astype(jnp.float32)
    rad_sin = rad_sin.astype(jnp.float32)
    model_re = jnp.einsum('chk,khp->ckp', smooth_re, rad_cos) - jnp.einsum('chk,khp->ckp', smooth_im, rad_sin)
    model_im = jnp.einsum('chk,khp->ckp', smooth_re, rad_sin) + jnp.einsum('chk,khp->ckp', smooth_im, rad_cos)
    power = model_re * model_re + model_im * model_im
    levels = shrink_level[None, :, None]
    mask_p = (jnp.arange(NP) >= NP // 4).astype(jnp.float32)
    factor = power / (power + levels * levels) * mask_p
    kept_re = (model_re * factor).astype(jnp.bfloat16).astype(jnp.float32)
    kept_im = (model_im * factor).astype(jnp.bfloat16).astype(jnp.float32)
    mult_re = jnp.einsum('ckp,khp->chk', kept_re, rad_cos) + jnp.einsum('ckp,khp->chk', kept_im, rad_sin)
    mult_im = jnp.einsum('ckp,khp->chk', kept_im, rad_cos) - jnp.einsum('ckp,khp->chk', kept_re, rad_sin)
    clean_re = (gather_re.astype(jnp.float32) - mult_re).astype(jnp.bfloat16)
    clean_im = (gather_im.astype(jnp.float32) - mult_im).astype(jnp.bfloat16)
    back_re = clean_re[mids, offs]
    back_im = clean_im[mids, offs]
    total = jnp.dot(back_re, cos_tab.T, preferred_element_type=jnp.float32) + jnp.dot(back_im, sin_tab.T, preferred_element_type=jnp.float32)
    return (2.0 * total).astype(jnp.bfloat16).reshape(N_OFF, TRH, NT)
```

```python
import functools
import math

import jax
import jax.numpy as jnp
import numpy as np
from jax import lax
from jax.experimental import pallas as pl
from jax.experimental.pallas import tpu as pltpu
from jax.sharding import PartitionSpec as P

NOFF = 128
NP = 128
radon_period = 4096
VMEM = pl.BlockSpec(memory_space=pltpu.VMEM)
ANY = pl.BlockSpec(memory_space=pl.ANY)


def dft_table(n_time, n_bands, band_size):
    sample = np.arange(n_time, dtype=np.int64)[:, None]
    freq_index = np.arange(n_bands * band_size, dtype=np.int64)[None, :]
    angle = 2.0 * np.pi * (sample * freq_index % n_time) / n_time
    scale_f = 1.0 / math.sqrt(n_time)
    cosine = (np.cos(angle) * scale_f).reshape(n_time, n_bands, band_size)
    sine = (-np.sin(angle) * scale_f).reshape(n_time, n_bands, band_size)
    table = np.stack([cosine, sine], axis=2).reshape(n_time, n_bands * 2 * band_size)
    return table.astype(np.float32).astype(jnp.bfloat16)


def radon_table(n_freqs, n_off):
    freq_index = np.arange(n_freqs, dtype=np.int64)[:, None, None]
    offset_index = np.arange(NOFF, dtype=np.int64)[None, :, None]
    slowness = np.arange(NP, dtype=np.int64)[None, None, :]
    turns = freq_index * slowness % radon_period * (offset_index * offset_index % radon_period) % radon_period
    circle = 2.0 * np.pi * np.arange(radon_period) / radon_period
    scale_r = 1.0 / math.sqrt(NOFF)
    cosine = (np.cos(circle) * scale_r).astype(np.float32).astype(jnp.bfloat16)[turns]
    sine = (np.sin(circle) * scale_r).astype(np.float32).astype(jnp.bfloat16)[turns]
    both = np.stack([cosine, sine], axis=1).reshape(n_freqs, 2, n_off, NOFF // n_off, NP)
    return np.ascontiguousarray(both.transpose(2, 0, 1, 3, 4)).reshape(n_off, n_freqs, 2 * NOFF // n_off, NP)


def signal(barrier, **device):
    pl.semaphore_signal(barrier, inc=1, device_id=device, device_id_type=pl.DeviceIdType.MESH)


def send(src, dst, send_sem, recv_sem, **device):
    return pltpu.make_async_remote_copy(
        src_ref=src,
        dst_ref=dst,
        send_sem=send_sem,
        recv_sem=recv_sem,
        device_id=device,
        device_id_type=pl.DeviceIdType.MESH,
    )


def spread_kernel(n_mid, n_freq, blocks, rows, own_sem, x_send, x_recv, z_send, z_recv):
    mid = lax.axis_index("mid")
    freq = lax.axis_index("freq")
    has = (mid < n_mid - 1, mid > 0)
    barrier = pltpu.get_barrier_semaphore()
    for d in range(1, n_freq):
        signal(barrier, freq=(freq + d) % n_freq)
    for way, step in ((0, 1), (1, -1)):

        @pl.when(has[way])
        def _():
            signal(barrier, mid=mid + step)

    pl.semaphore_wait(barrier, n_freq - 1 + has[0].astype(jnp.int32) + has[1].astype(jnp.int32))
    own = pltpu.make_async_copy(blocks.at[freq], rows.at[mid, freq], own_sem)
    own.start()
    across = []
    for d in range(1, n_freq):
        other = (freq + d) % n_freq
        across.append(send(blocks.at[other], rows.at[mid, freq], x_send.at[d], x_recv.at[d], freq=other))
        across[-1].start()

    def hop(way, step, s, d):
        start = mid - step * s
        origin = (freq + n_freq - d) % n_freq
        src = blocks.at[freq] if s == 0 and d == 0 else rows.at[start, origin]
        return send(src, rows.at[start, origin], z_send.at[way, s, d], z_recv.at[way, s, d], mid=mid + step)

    for s in range(n_mid):
        for d in range(n_freq):
            if s == 0 and d > 0:
                across[d - 1].wait_recv()
            for way, step in ((0, 1), (1, -1)):
                behind = mid - step * s
                real = (behind >= 0) & (behind < n_mid)
                if s > 0:

                    @pl.when(real)
                    def _():
                        hop(way, step, s - 1, d).wait_recv()

                if s < n_mid - 1:

                    @pl.when(real & has[way])
                    def _():
                        hop(way, step, s, d).start()

    own.wait()
    for copy in across:
        copy.wait_send()
    for s in range(n_mid - 1):
        for d in range(n_freq):
            for way, step in ((0, 1), (1, -1)):
                behind = mid - step * s

                @pl.when((behind >= 0) & (behind < n_mid) & has[way])
                def _():
                    hop(way, step, s, d).wait_send()


def spread(blocks, n_mid):
    n_freq = blocks.shape[0]
    return pl.pallas_call(
        functools.partial(spread_kernel, n_mid, n_freq),
        out_shape=jax.ShapeDtypeStruct((n_mid,) + blocks.shape, blocks.dtype),
        in_specs=[VMEM],
        out_specs=VMEM,
        scratch_shapes=[
            pltpu.SemaphoreType.DMA,
            pltpu.SemaphoreType.DMA((n_freq,)),
            pltpu.SemaphoreType.DMA((n_freq,)),
            pltpu.SemaphoreType.DMA((2, n_mid, n_freq)),
            pltpu.SemaphoreType.DMA((2, n_mid, n_freq)),
        ],
        compiler_params=pltpu.CompilerParams(collective_id=0, has_side_effects=True),
    )(blocks)


def return_kernel(n_mid, n_freq, blocks, got, own_sem, send_sem, recv_sem):
    mid = lax.axis_index("mid")
    freq = lax.axis_index("freq")
    others = [(a, b) for a in range(n_mid) for b in range(n_freq) if (a, b) != (0, 0)]
    barrier = pltpu.get_barrier_semaphore()
    for a, b in others:
        signal(barrier, mid=(mid + a) % n_mid, freq=(freq + b) % n_freq)
    pl.semaphore_wait(barrier, len(others))
    copies = []
    for a, b in others:
        to_mid, to_freq = (mid + a) % n_mid, (freq + b) % n_freq
        copies.append(
            send(
                blocks.at[to_mid, to_freq],
                got.at[mid, freq],
                send_sem.at[a, b],
                recv_sem.at[a, b],
                mid=to_mid,
                freq=to_freq,
            )
        )
        copies[-1].start()
    own = pltpu.make_async_copy(blocks.at[mid, freq], got.at[mid, freq], own_sem)
    own.start()
    own.wait()
    for copy in copies:
        copy.wait()


def give_back(blocks):
    n_mid, n_freq = blocks.shape[:2]
    return pl.pallas_call(
        functools.partial(return_kernel, n_mid, n_freq),
        out_shape=jax.ShapeDtypeStruct(blocks.shape, blocks.dtype),
        in_specs=[VMEM],
        out_specs=VMEM,
        scratch_shapes=[
            pltpu.SemaphoreType.DMA,
            pltpu.SemaphoreType.DMA((n_mid, n_freq)),
            pltpu.SemaphoreType.DMA((n_mid, n_freq)),
        ],
        compiler_params=pltpu.CompilerParams(collective_id=1, has_side_effects=True),
    )(blocks)


def radon_kernel(n_off, chunk, x, level, table, out, weights, part, got, t_sem, send_sem, recv_sem):
    freq = lax.axis_index("freq")
    off = lax.axis_index("off")
    band, rows, width = x.shape
    half = rows // 2
    n_chunks = band // chunk

    def span(j):
        return pl.ds(pl.multiple_of(j * chunk, chunk), chunk)

    def fetch(j):
        first = pl.multiple_of(freq * band + j * chunk, chunk)
        return pltpu.make_async_copy(table.at[off, pl.ds(first, chunk)], weights.at[span(j)], t_sem.at[j])

    def pass_on(j, d):
        return send(
            part.at[span(j)],
            got.at[d - 1, span(j)],
            send_sem.at[d - 1, j],
            recv_sem.at[d - 1, j],
            off=(off + d) % n_off,
        )

    @pl.loop(0, n_chunks)
    def _(j):
        fetch(j).start()

    barrier = pltpu.get_barrier_semaphore()
    for d in range(1, n_off):
        signal(barrier, off=(off + d) % n_off)
    pl.semaphore_wait(barrier, n_off - 1)

    @pl.loop(0, n_chunks)
    def _(j):
        fetch(j).wait()
        part[span(j)] = lax.dot_general(
            x[span(j)], weights[span(j)], (((2,), (1,)), ((0,), (0,))), preferred_element_type=jnp.float32
        )
        for d in range(1, n_off):
            pass_on(j, d).start()

    keep = (lax.broadcasted_iota(jnp.int32, (chunk, rows, NP), 2) >= NP // 4).astype(jnp.float32)

    @pl.loop(0, n_chunks)
    def _(j):
        model = part[span(j)]
        for d in range(1, n_off):
            pass_on(j, d).wait_recv()
            model = model + got[d - 1, span(j)]
        squares = model * model
        power = squares + pltpu.roll(squares, half, 1)
        lev = level[span(j)]
        factor = power / (power + lev * lev) * keep
        kept = (model * factor).astype(jnp.bfloat16)
        both = lax.dot_general(
            kept, weights[span(j)], (((2,), (2,)), ((0,), (0,))), preferred_element_type=jnp.float32
        )
        out[span(j)] = both + pltpu.roll(pltpu.roll(both, half, 1), width // 2, 2)

    @pl.loop(0, n_chunks)
    def _(j):
        for d in range(1, n_off):
            pass_on(j, d).wait_send()


def radon(x, level, table, n_off):
    band, rows, width = x.shape
    chunk = min(32, band)
    n_chunks = band // chunk
    return pl.pallas_call(
        functools.partial(radon_kernel, n_off, chunk),
        out_shape=jax.ShapeDtypeStruct(x.shape, jnp.float32),
        in_specs=[VMEM, VMEM, ANY],
        out_specs=VMEM,
        scratch_shapes=[
            pltpu.VMEM((band, width, NP), jnp.bfloat16),
            pltpu.VMEM((band, rows, NP), jnp.float32),
            pltpu.VMEM((n_off - 1, band, rows, NP), jnp.float32),
            pltpu.SemaphoreType.DMA((n_chunks,)),
            pltpu.SemaphoreType.DMA((n_off - 1, n_chunks)),
            pltpu.SemaphoreType.DMA((n_off - 1, n_chunks)),
        ],
        compiler_params=pltpu.CompilerParams(
            collective_id=2, has_side_effects=True, vmem_limit_bytes=32 * 1024 * 1024
        ),
    )(x, level, table)


def on_device(dft, weights, traces, time_filter, midpoint_of, offset_of, shrink_level):
    n_mid = lax.axis_size("mid")
    n_freq = lax.axis_size("freq")
    n_off = lax.axis_size("off")
    me_mid = lax.axis_index("mid")
    me_freq = lax.axis_index("freq")
    me_off = lax.axis_index("off")
    tr_dev = traces.shape[1]
    band = shrink_level.shape[0]
    noff_dev = NOFF // n_off
    cmp_dev = n_freq * tr_dev // noff_dev
    capacity = 2 * tr_dev // n_mid
    n_send = n_mid * n_freq
    n_cells = cmp_dev * noff_dev
    width = 2 * band
    f32, bf16 = jnp.float32, jnp.bfloat16

    filtered = jnp.dot(traces[0], time_filter, preferred_element_type=f32).astype(bf16)
    spectra = jnp.dot(filtered, dft, preferred_element_type=f32).astype(bf16)
    blocks = jnp.transpose(spectra.reshape(tr_dev, n_freq, width), (1, 0, 2))
    rows = spread(blocks, n_mid).reshape(n_send * tr_dev, width)

    mids = midpoint_of[0]
    offs = offset_of[0] % noff_dev
    cell = jnp.arange(n_cells, dtype=jnp.int32)[:, None]
    apart = jnp.abs(mids[None, :] - (me_mid * cmp_dev + cell // noff_dev))
    hit = offs[None, :] == cell % noff_dev
    mix = jnp.where(hit & (apart < 2), jnp.where(apart == 0, 0.5, 0.25), 0.0).astype(bf16)
    smooth = jnp.dot(mix, rows, preferred_element_type=f32).astype(bf16)
    smooth = jnp.transpose(smooth.reshape(cmp_dev, noff_dev, 2, band), (3, 2, 0, 1))
    re, im = smooth[:, 0], smooth[:, 1]
    first = jnp.concatenate([re, -im], axis=2)
    second = jnp.concatenate([im, re], axis=2)
    x = jnp.concatenate([first, second, second, -first], axis=1)
    level = jnp.broadcast_to(shrink_level[:, None, None], (band, 1, NP))
    mult = radon(x, level, weights, n_off)
    mult = mult[:, : 2 * cmp_dev, :noff_dev].astype(bf16).reshape(band, 2, cmp_dev, noff_dev)
    mult = jnp.transpose(mult, (2, 3, 1, 0)).reshape(n_cells, width)

    owner = (mids // cmp_dev).reshape(n_send, tr_dev)
    trace_cell = (mids % cmp_dev * noff_dev + offs).reshape(n_send, tr_dev)
    place = jnp.arange(tr_dev, dtype=jnp.int32)
    before = (owner[:, :, None] == owner[:, None, :]) & (place[None, None, :] < place[None, :, None])
    rank = jnp.sum(before.astype(jnp.int32), axis=2)
    slots = jnp.arange(capacity, dtype=jnp.int32)
    mine = (owner == me_mid)[:, None, :] & (rank[:, None, :] == slots[None, :, None])
    slot_cell = jnp.sum(jnp.where(mine, trace_cell[:, None, :] + 1, 0), axis=2) - 1
    pick = (slot_cell.reshape(-1)[:, None] == jnp.arange(n_cells, dtype=jnp.int32)[None, :]).astype(bf16)
    back = jnp.dot(pick, mult, preferred_element_type=f32).astype(bf16)
    returned = give_back(back.reshape(n_mid, n_freq, capacity, width))

    me = me_mid * n_freq + me_freq
    own_slot = owner[me] * capacity + rank[me]
    take = (own_slot[:, None] == jnp.arange(n_mid * capacity, dtype=jnp.int32)[None, :]).astype(bf16)
    ordered = jnp.transpose(returned, (0, 2, 1, 3)).reshape(n_mid * capacity, n_freq * width)
    own_mult = jnp.dot(take, ordered, preferred_element_type=f32)
    clean = (spectra.astype(f32) - own_mult).astype(bf16)
    total = lax.dot_general(clean, dft, (((1,), (1,)), ((), ())), preferred_element_type=f32)
    return (2.0 * total).astype(bf16)[None]


def solution(mesh):
    n_freq = mesh.shape["freq"]

    def run(traces, time_filter, midpoint_of, offset_of, shrink_level):
        n_freqs = shrink_level.shape[0]
        dft = dft_table(traces.shape[2], n_freq, n_freqs // n_freq)
        weights = radon_table(n_freqs, mesh.shape["off"])
        return jax.shard_map(
            on_device,
            mesh=mesh,
            in_specs=(
                P(),
                P(),
                P("off", ("group", "mid", "freq"), None),
                P(),
                P("off", "group"),
                P("off", "group"),
                P("freq"),
            ),
            out_specs=P("off", ("group", "mid", "freq"), None),
            check_vma=False,
        )(jnp.asarray(dft), jnp.asarray(weights), traces, time_filter, midpoint_of, offset_of, shrink_level)

    return run
```

```python
import functools
import math

import jax
import jax.numpy as jnp
import numpy as np
from jax import lax
from jax.experimental import pallas as pl
from jax.experimental.pallas import tpu as pltpu
from jax.sharding import PartitionSpec as P

NOFF = 128
NP = 128
radon_period = 4096
VMEM = pl.BlockSpec(memory_space=pltpu.VMEM)
ANY = pl.BlockSpec(memory_space=pl.ANY)


def dft_table(n_time, n_bands, band_size):
    sample = np.arange(n_time, dtype=np.int64)[:, None]
    freq_index = np.arange(n_bands * band_size, dtype=np.int64)[None, :]
    angle = 2.0 * np.pi * (sample * freq_index % n_time) / n_time
    scale_f = 1.0 / math.sqrt(n_time)
    cosine = (np.cos(angle) * scale_f).reshape(n_time, n_bands, band_size)
    sine = (-np.sin(angle) * scale_f).reshape(n_time, n_bands, band_size)
    table = np.stack([cosine, sine], axis=2).reshape(n_time, n_bands * 2 * band_size)
    return table.astype(np.float32).astype(jnp.bfloat16)


def radon_table(n_freqs):
    freq_index = np.arange(n_freqs, dtype=np.int64)[:, None, None]
    offset_index = np.arange(NOFF, dtype=np.int64)[None, :, None]
    slowness = np.arange(NP, dtype=np.int64)[None, None, :]
    turns = freq_index * slowness % radon_period * (offset_index * offset_index % radon_period) % radon_period
    circle = 2.0 * np.pi * np.arange(radon_period) / radon_period
    scale_r = 1.0 / math.sqrt(NOFF)
    cosine = (np.cos(circle) * scale_r).astype(np.float32).astype(jnp.bfloat16)[turns]
    sine = (np.sin(circle) * scale_r).astype(np.float32).astype(jnp.bfloat16)[turns]
    return np.stack([cosine, sine], axis=1).reshape(n_freqs, 2 * NOFF, NP)


def signal(barrier, **device):
    pl.semaphore_signal(barrier, inc=1, device_id=device, device_id_type=pl.DeviceIdType.MESH)


def send(src, dst, send_sem, recv_sem, **device):
    return pltpu.make_async_remote_copy(
        src_ref=src,
        dst_ref=dst,
        send_sem=send_sem,
        recv_sem=recv_sem,
        device_id=device,
        device_id_type=pl.DeviceIdType.MESH,
    )


def place(sizes):
    names = ("off", "mid", "freq")
    here = [lax.axis_index(name) for name in names]
    index = (here[0] * sizes[1] + here[1]) * sizes[2] + here[2]
    total = sizes[0] * sizes[1] * sizes[2]

    def ahead(i):
        there = (index + i) % total
        return there, dict(off=there // (sizes[1] * sizes[2]), mid=there // sizes[2] % sizes[1], freq=there % sizes[2])

    return index, total, ahead


def swap_kernel(sizes, with_ids, *refs):
    if with_ids:
        blocks, ids, got, got_ids, own_sem, send_sem, recv_sem, id_own, id_send, id_recv = refs
    else:
        blocks, got, own_sem, send_sem, recv_sem = refs
    index, total, ahead = place(sizes)
    n_off = sizes[0]
    barrier = pltpu.get_barrier_semaphore()

    @pl.loop(1, total)
    def _(i):
        signal(barrier, **ahead(i)[1])

    own = pltpu.make_async_copy(blocks.at[index], got.at[index], own_sem)
    own.start()
    pl.semaphore_wait(barrier, total - 1)

    def block_copy(i):
        there, device = ahead(i)
        return send(blocks.at[there], got.at[index], send_sem.at[i], recv_sem.at[i], **device)

    def id_copy(d):
        off = lax.axis_index("off")
        return send(ids, got_ids.at[off], id_send.at[d], id_recv.at[d], off=(off + d) % n_off)

    if with_ids:
        own_ids = pltpu.make_async_copy(ids, got_ids.at[lax.axis_index("off")], id_own)
        own_ids.start()
        for d in range(1, n_off):
            id_copy(d).start()

    @pl.loop(1, total)
    def _(i):
        block_copy(i).start()

    own.wait()
    if with_ids:
        own_ids.wait()
        for d in range(1, n_off):
            id_copy(d).wait()

    @pl.loop(1, total)
    def _(i):
        block_copy(i).wait()


def swap(blocks, sizes, collective_id, ids=None):
    total, n_off = blocks.shape[0], sizes[0]
    dma = pltpu.SemaphoreType.DMA
    shapes = [jax.ShapeDtypeStruct(blocks.shape, blocks.dtype)]
    scratch = [dma, dma((total,)), dma((total,))]
    operands = [blocks]
    if ids is not None:
        shapes.append(jax.ShapeDtypeStruct((n_off,) + ids.shape, ids.dtype))
        scratch += [dma, dma((n_off,)), dma((n_off,))]
        operands.append(ids)
    return pl.pallas_call(
        functools.partial(swap_kernel, sizes, ids is not None),
        out_shape=shapes,
        in_specs=[VMEM] * len(operands),
        out_specs=[VMEM] * len(shapes),
        scratch_shapes=scratch,
        compiler_params=pltpu.CompilerParams(collective_id=collective_id, has_side_effects=True),
    )(*operands)


def radon_kernel(n_mid, n_off, smooth, level, table, out, weights, sem):
    count, mids = smooth.shape[1:3]
    q = (lax.axis_index("freq") * n_mid + lax.axis_index("mid")) * n_off + lax.axis_index("off")
    fetch = pltpu.make_async_copy(table.at[pl.ds(q * count, count)], weights, sem)
    fetch.start()
    re = smooth[0].astype(jnp.float32)
    im = smooth[1].astype(jnp.float32)
    first = jnp.concatenate([re, -im], axis=2)
    second = jnp.concatenate([im, re], axis=2)
    x = jnp.concatenate([first, second], axis=1).astype(jnp.bfloat16)
    fetch.wait()
    model = lax.dot_general(x, weights[...], (((2,), (1,)), ((0,), (0,))), preferred_element_type=jnp.float32)
    model_re, model_im = model[:, :mids], model[:, mids:]
    power = model_re * model_re + model_im * model_im
    keep = (lax.broadcasted_iota(jnp.int32, power.shape, 2) >= NP // 4).astype(jnp.float32)
    lev = level[...]
    factor = power / (power + lev * lev) * keep
    kept = jnp.concatenate([model_re * factor, model_im * factor], axis=1).astype(jnp.bfloat16)
    both = lax.dot_general(kept, weights[...], (((2,), (2,)), ((0,), (0,))), preferred_element_type=jnp.float32)
    out[0] = (both[:, :mids, :NOFF] + both[:, mids:, NOFF:]).astype(jnp.bfloat16)
    out[1] = (both[:, mids:, :NOFF] - both[:, :mids, NOFF:]).astype(jnp.bfloat16)


def radon(smooth, level, table, n_mid, n_off):
    count = smooth.shape[1]
    return pl.pallas_call(
        functools.partial(radon_kernel, n_mid, n_off),
        out_shape=jax.ShapeDtypeStruct(smooth.shape, jnp.bfloat16),
        in_specs=[VMEM, VMEM, ANY],
        out_specs=VMEM,
        scratch_shapes=[pltpu.VMEM((count, 2 * NOFF, NP), jnp.bfloat16), pltpu.SemaphoreType.DMA],
        compiler_params=pltpu.CompilerParams(vmem_limit_bytes=24 * 1024 * 1024),
    )(smooth, level, table)


def on_device(dft, weights, traces, time_filter, midpoint_of, offset_of, shrink_level):
    n_mid = lax.axis_size("mid")
    n_freq = lax.axis_size("freq")
    n_off = lax.axis_size("off")
    sizes = (n_off, n_mid, n_freq)
    total = n_off * n_mid * n_freq
    me_mid = lax.axis_index("mid")
    me_off = lax.axis_index("off")
    tr_dev = traces.shape[1]
    count = shrink_level.shape[0] // (n_mid * n_off)
    width = 2 * count
    pack = max(1, min(tr_dev, 128 // width))
    n_traces = total * tr_dev
    n_mids = n_traces // NOFF
    f32, bf16 = jnp.float32, jnp.bfloat16

    filtered = jnp.dot(traces[0], time_filter, preferred_element_type=f32).astype(bf16)
    spectra = jnp.dot(filtered, dft, preferred_element_type=f32).astype(bf16)
    blocks = spectra.reshape(pack, tr_dev // pack, total, width)
    blocks = jnp.transpose(blocks, (2, 1, 0, 3)).reshape(total, tr_dev // pack, pack * width)
    rows, ids = swap(blocks, sizes, 0, midpoint_of * NOFF + offset_of)
    rows = rows.reshape(total, tr_dev // pack, pack, width)
    rows = jnp.transpose(rows, (0, 2, 1, 3)).reshape(n_traces, width)
    cell_of = ids.reshape(n_traces)

    small = n_traces <= 4096
    if small:
        cells = jnp.arange(n_traces, dtype=jnp.int32)[None, :]
        away = jnp.abs(cell_of[:, None] - cells)
        mix = jnp.where(away == 0, 0.5, jnp.where(away == NOFF, 0.25, 0.0)).astype(bf16)
        smooth = lax.dot_general(rows, mix, (((0,), (0,)), ((), ())), preferred_element_type=f32)
        smooth = smooth.astype(bf16).reshape(2, count, n_mids, NOFF)
    else:
        gather = jnp.zeros((n_traces, width), bf16).at[cell_of].set(rows)
        edged = jnp.pad(gather.reshape(n_mids, NOFF, 2, count).astype(f32), ((1, 1), (0, 0), (0, 0), (0, 0)))
        smooth = ((edged[:-2] + 2.0 * edged[1:-1] + edged[2:]) * 0.25).astype(bf16)
        smooth = jnp.transpose(smooth, (2, 3, 0, 1))
    own_levels = lax.dynamic_slice_in_dim(shrink_level, (me_mid * n_off + me_off) * count, count)
    level = jnp.broadcast_to(own_levels[:, None, None], (count, 1, NP))
    mult = radon(smooth, level, weights, n_mid, n_off).reshape(width, n_traces)
    if small:
        pick = (cell_of[:, None] == cells).astype(bf16)
        back = lax.dot_general(pick, mult, (((1,), (1,)), ((), ())), preferred_element_type=f32).astype(bf16)
    else:
        back = jnp.transpose(mult)[cell_of]
    back = back.reshape(total, pack, tr_dev // pack, width)
    back = jnp.transpose(back, (0, 2, 1, 3)).reshape(total, tr_dev // pack, pack * width)
    (returned,) = swap(back, sizes, 1)
    returned = returned.reshape(total, tr_dev // pack, pack, width)
    own_mult = jnp.transpose(returned, (2, 1, 0, 3)).reshape(tr_dev, total * width)
    clean = (spectra.astype(f32) - own_mult.astype(f32)).astype(bf16)
    sums = lax.dot_general(clean, dft, (((1,), (1,)), ((), ())), preferred_element_type=f32)
    return (2.0 * sums).astype(bf16)[None]


def solution(mesh):
    n_freq, n_mid, n_off = (mesh.shape[name] for name in ("freq", "mid", "off"))

    def run(traces, time_filter, midpoint_of, offset_of, shrink_level):
        n_freqs = shrink_level.shape[0]
        n_time = traces.shape[2]
        pieces = n_freq * n_mid * n_off
        dft = dft_table(n_time, pieces, n_freqs // pieces).reshape(n_time, n_freq, n_mid, n_off, -1)
        dft = np.ascontiguousarray(dft.transpose(0, 3, 2, 1, 4)).reshape(n_time, 2 * n_freqs)
        weights = radon_table(n_freqs)
        return jax.shard_map(
            on_device,
            mesh=mesh,
            in_specs=(
                P(),
                P(),
                P("off", ("group", "mid", "freq"), None),
                P(),
                P("off", "group"),
                P("off", "group"),
                P("freq"),
            ),
            out_specs=P("off", ("group", "mid", "freq"), None),
            check_vma=False,
        )(jnp.asarray(dft), jnp.asarray(weights), traces, time_filter, midpoint_of, offset_of, shrink_level)

    return run
```

```python
import functools
import math

import jax
import jax.numpy as jnp
import numpy as np
from jax import lax
from jax.experimental import pallas as pl
from jax.experimental.pallas import tpu as pltpu
from jax.sharding import PartitionSpec as P

NOFF = 128
NP = 128
radon_period = 4096
VMEM = pl.BlockSpec(memory_space=pltpu.VMEM)
ANY = pl.BlockSpec(memory_space=pl.ANY)


def dft_table(n_time, n_bands, band_size):
    sample = np.arange(n_time, dtype=np.int64)[:, None]
    freq_index = np.arange(n_bands * band_size, dtype=np.int64)[None, :]
    angle = 2.0 * np.pi * (sample * freq_index % n_time) / n_time
    scale_f = 1.0 / math.sqrt(n_time)
    cosine = (np.cos(angle) * scale_f).reshape(n_time, n_bands, band_size)
    sine = (-np.sin(angle) * scale_f).reshape(n_time, n_bands, band_size)
    table = np.stack([cosine, sine], axis=2).reshape(n_time, n_bands * 2 * band_size)
    return table.astype(np.float32).astype(jnp.bfloat16)


def radon_table(n_freqs):
    freq_index = np.arange(n_freqs, dtype=np.int64)[:, None, None]
    offset_index = np.arange(NOFF, dtype=np.int64)[None, :, None]
    slowness = np.arange(NP, dtype=np.int64)[None, None, :]
    turns = freq_index * slowness % radon_period * (offset_index * offset_index % radon_period) % radon_period
    circle = 2.0 * np.pi * np.arange(radon_period) / radon_period
    scale_r = 1.0 / math.sqrt(NOFF)
    cosine = (np.cos(circle) * scale_r).astype(np.float32).astype(jnp.bfloat16)[turns]
    sine = (np.sin(circle) * scale_r).astype(np.float32).astype(jnp.bfloat16)[turns]
    return np.stack([cosine, sine], axis=1).reshape(n_freqs, 2 * NOFF, NP)


def signal(barrier, **device):
    pl.semaphore_signal(barrier, inc=1, device_id=device, device_id_type=pl.DeviceIdType.MESH)


def send(src, dst, send_sem, recv_sem, **device):
    return pltpu.make_async_remote_copy(
        src_ref=src,
        dst_ref=dst,
        send_sem=send_sem,
        recv_sem=recv_sem,
        device_id=device,
        device_id_type=pl.DeviceIdType.MESH,
    )


def place(sizes):
    names = ("off", "mid", "freq")
    here = [lax.axis_index(name) for name in names]
    index = (here[0] * sizes[1] + here[1]) * sizes[2] + here[2]
    total = sizes[0] * sizes[1] * sizes[2]

    def ahead(i):
        there = (index + i) % total
        return there, dict(off=there // (sizes[1] * sizes[2]), mid=there // sizes[2] % sizes[1], freq=there % sizes[2])

    return index, total, ahead


def swap_kernel(sizes, with_ids, *refs):
    if with_ids:
        blocks, ids, got, got_ids, own_sem, send_sem, recv_sem, id_own, id_send, id_recv = refs
    else:
        blocks, got, own_sem, send_sem, recv_sem = refs
    index, total, ahead = place(sizes)
    n_off = sizes[0]
    barrier = pltpu.get_barrier_semaphore()

    @pl.loop(1, total)
    def _(i):
        signal(barrier, **ahead(i)[1])

    own = pltpu.make_async_copy(blocks.at[index], got.at[index], own_sem)
    own.start()
    pl.semaphore_wait(barrier, total - 1)

    def block_copy(i):
        there, device = ahead(i)
        return send(blocks.at[there], got.at[index], send_sem.at[i], recv_sem.at[i], **device)

    def id_copy(d):
        off = lax.axis_index("off")
        return send(ids, got_ids.at[off], id_send.at[d], id_recv.at[d], off=(off + d) % n_off)

    if with_ids:
        own_ids = pltpu.make_async_copy(ids, got_ids.at[lax.axis_index("off")], id_own)
        own_ids.start()
        for d in range(1, n_off):
            id_copy(d).start()

    @pl.loop(1, total)
    def _(i):
        block_copy(i).start()

    own.wait()
    if with_ids:
        own_ids.wait()
        for d in range(1, n_off):
            id_copy(d).wait()

    @pl.loop(1, total)
    def _(i):
        block_copy(i).wait()


def swap(blocks, sizes, collective_id, ids=None):
    total, n_off = blocks.shape[0], sizes[0]
    dma = pltpu.SemaphoreType.DMA
    shapes = [jax.ShapeDtypeStruct(blocks.shape, blocks.dtype)]
    scratch = [dma, dma((total,)), dma((total,))]
    operands = [blocks]
    if ids is not None:
        shapes.append(jax.ShapeDtypeStruct((n_off,) + ids.shape, ids.dtype))
        scratch += [dma, dma((n_off,)), dma((n_off,))]
        operands.append(ids)
    return pl.pallas_call(
        functools.partial(swap_kernel, sizes, ids is not None),
        out_shape=shapes,
        in_specs=[VMEM] * len(operands),
        out_specs=[VMEM] * len(shapes),
        scratch_shapes=scratch,
        compiler_params=pltpu.CompilerParams(collective_id=collective_id, has_side_effects=True),
    )(*operands)


def radon_kernel(n_mid, n_off, smooth, level, table, out, weights, sem):
    count, mids = smooth.shape[1:3]
    q = (lax.axis_index("freq") * n_mid + lax.axis_index("mid")) * n_off + lax.axis_index("off")
    fetch = pltpu.make_async_copy(table.at[pl.ds(q * count, count)], weights, sem)
    fetch.start()
    re = smooth[0].astype(jnp.float32)
    im = smooth[1].astype(jnp.float32)
    first = jnp.concatenate([re, -im], axis=2)
    second = jnp.concatenate([im, re], axis=2)
    x = jnp.concatenate([first, second], axis=1).astype(jnp.bfloat16)
    fetch.wait()
    model = lax.dot_general(x, weights[...], (((2,), (1,)), ((0,), (0,))), preferred_element_type=jnp.float32)
    model_re, model_im = model[:, :mids], model[:, mids:]
    power = model_re * model_re + model_im * model_im
    keep = (lax.broadcasted_iota(jnp.int32, power.shape, 2) >= NP // 4).astype(jnp.float32)
    lev = level[...]
    factor = power / (power + lev * lev) * keep
    kept = jnp.concatenate([model_re * factor, model_im * factor], axis=1).astype(jnp.bfloat16)
    both = lax.dot_general(kept, weights[...], (((2,), (2,)), ((0,), (0,))), preferred_element_type=jnp.float32)
    out[0] = (both[:, :mids, :NOFF] + both[:, mids:, NOFF:]).astype(jnp.bfloat16)
    out[1] = (both[:, mids:, :NOFF] - both[:, :mids, NOFF:]).astype(jnp.bfloat16)


def radon(smooth, level, table, n_mid, n_off):
    count = smooth.shape[1]
    return pl.pallas_call(
        functools.partial(radon_kernel, n_mid, n_off),
        out_shape=jax.ShapeDtypeStruct(smooth.shape, jnp.bfloat16),
        in_specs=[VMEM, VMEM, ANY],
        out_specs=VMEM,
        scratch_shapes=[pltpu.VMEM((count, 2 * NOFF, NP), jnp.bfloat16), pltpu.SemaphoreType.DMA],
        compiler_params=pltpu.CompilerParams(vmem_limit_bytes=24 * 1024 * 1024),
    )(smooth, level, table)


def fused_kernel(sizes, pack, blocks, ids, level, table, ret, got, got_ids, back, weights, near, same, cube, t_sem, own_sem, send_sem, recv_sem, id_own, id_send, id_recv):
    index, total, ahead = place(sizes)
    n_off, n_mid, n_freq = sizes
    off = lax.axis_index("off")
    f32, bf16 = jnp.float32, jnp.bfloat16
    width, mids = cube.shape[:2]
    count = width // 2
    n_cells = mids * NOFF
    per_half = ids.shape[1]
    barrier = pltpu.get_barrier_semaphore()

    @pl.loop(1, total)
    def _(i):
        signal(barrier, **ahead(i)[1])

    q = (lax.axis_index("freq") * n_mid + lax.axis_index("mid")) * n_off + off
    fetch = pltpu.make_async_copy(table.at[pl.ds(q * count, count)], weights, t_sem)
    fetch.start()
    own = pltpu.make_async_copy(blocks.at[index], got.at[index], own_sem.at[0])
    own.start()
    own_ids = pltpu.make_async_copy(ids, got_ids.at[off], id_own)
    own_ids.start()
    pl.semaphore_wait(barrier, total - 1)

    def block_copy(way, src, dst, i):
        there, device = ahead(i)
        return send(src.at[there], dst.at[index], send_sem.at[way, i], recv_sem.at[way, i], **device)

    def id_copy(d):
        return send(ids, got_ids.at[off], id_send.at[d], id_recv.at[d], off=(off + d) % n_off)

    for d in range(1, n_off):
        id_copy(d).start()

    @pl.loop(1, total)
    def _(i):
        block_copy(0, blocks, got, i).start()

    own_ids.wait()
    for d in range(1, n_off):
        id_copy(d).wait()
    step = 128

    @pl.loop(0, n_cells // step)
    def _(j):
        here = pl.multiple_of(j * step, step)
        cell = lax.broadcasted_iota(jnp.int32, (step, per_half), 0) + here
        for o in range(n_off):
            for pk in range(pack):
                away = jnp.abs(cell - got_ids[o, pl.ds(pk, 1), :])
                hit = jnp.where(away == 0, 1.0, 0.0)
                near[pk, o, pl.ds(here, step)] = (0.5 * hit + jnp.where(away == NOFF, 0.25, 0.0)).astype(bf16)
                same[pk, o, pl.ds(here, step)] = hit.astype(bf16)

    own.wait()

    @pl.loop(1, total)
    def _(i):
        block_copy(0, blocks, got, i).wait()

    rows = jnp.transpose(got[...].reshape(n_off * per_half, pack * width).astype(f32)).astype(bf16)
    smooth = jnp.zeros((width, n_cells), f32)
    for pk in range(pack):
        for o in range(n_off):
            smooth += lax.dot_general(
                rows[pk * width : (pk + 1) * width, o * per_half : (o + 1) * per_half],
                near[pk, o],
                (((1,), (1,)), ((), ())),
                preferred_element_type=f32,
            )
    for c in range(mids):
        cube[:, c, :] = smooth[:, c * NOFF : (c + 1) * NOFF]
    re, im = cube[pl.ds(0, count)], cube[pl.ds(count, count)]
    first = jnp.concatenate([re, -im], axis=2)
    second = jnp.concatenate([im, re], axis=2)
    x = jnp.concatenate([first, second], axis=1).astype(bf16)
    fetch.wait()
    model = lax.dot_general(x, weights[...], (((2,), (1,)), ((0,), (0,))), preferred_element_type=f32)
    model_re, model_im = model[:, :mids], model[:, mids:]
    power = model_re * model_re + model_im * model_im
    keep = (lax.broadcasted_iota(jnp.int32, power.shape, 2) >= NP // 4).astype(f32)
    lev = level[...]
    factor = power / (power + lev * lev) * keep
    kept = jnp.concatenate([model_re * factor, model_im * factor], axis=1).astype(bf16)
    both = lax.dot_general(kept, weights[...], (((2,), (2,)), ((0,), (0,))), preferred_element_type=f32)
    cube[pl.ds(0, count)] = both[:, :mids, :NOFF] + both[:, mids:, NOFF:]
    cube[pl.ds(count, count)] = both[:, mids:, :NOFF] - both[:, :mids, NOFF:]
    mult = jnp.concatenate([cube[:, c, :] for c in range(mids)], axis=1).astype(bf16)
    for o in range(n_off):
        lines = [jnp.dot(mult, same[pk, o], preferred_element_type=f32) for pk in range(pack)]
        lines = jnp.transpose(jnp.concatenate(lines, axis=0)).astype(bf16)
        part = total // n_off
        back[pl.ds(o * part, part)] = lines.reshape((part,) + blocks.shape[1:])
    own_back = pltpu.make_async_copy(back.at[index], ret.at[index], own_sem.at[1])
    own_back.start()

    @pl.loop(1, total)
    def _(i):
        block_copy(1, back, ret, i).start()

    own_back.wait()

    @pl.loop(1, total)
    def _(i):
        block_copy(1, back, ret, i).wait()


def fused(blocks, ids, level, table, sizes, pack):
    total, n_off = blocks.shape[0], sizes[0]
    count = level.shape[0]
    per_half = ids.shape[1]
    n_cells = n_off * per_half * pack
    dma = pltpu.SemaphoreType.DMA
    bf16 = jnp.bfloat16
    return pl.pallas_call(
        functools.partial(fused_kernel, sizes, pack),
        out_shape=jax.ShapeDtypeStruct(blocks.shape, blocks.dtype),
        in_specs=[VMEM, VMEM, VMEM, ANY],
        out_specs=VMEM,
        scratch_shapes=[
            pltpu.VMEM(blocks.shape, bf16),
            pltpu.VMEM((n_off,) + ids.shape, jnp.int32),
            pltpu.VMEM(blocks.shape, bf16),
            pltpu.VMEM((count, 2 * NOFF, NP), bf16),
            pltpu.VMEM((pack, n_off, n_cells, per_half), bf16),
            pltpu.VMEM((pack, n_off, n_cells, per_half), bf16),
            pltpu.VMEM((2 * count, n_cells // NOFF, NOFF), jnp.float32),
            dma,
            dma((2,)),
            dma((2, total)),
            dma((2, total)),
            dma,
            dma((n_off,)),
            dma((n_off,)),
        ],
        compiler_params=pltpu.CompilerParams(
            collective_id=2, has_side_effects=True, vmem_limit_bytes=40 * 1024 * 1024
        ),
    )(blocks, ids, level, table)


def on_device(dft, weights, traces, time_filter, midpoint_of, offset_of, shrink_level):
    n_mid = lax.axis_size("mid")
    n_freq = lax.axis_size("freq")
    n_off = lax.axis_size("off")
    sizes = (n_off, n_mid, n_freq)
    total = n_off * n_mid * n_freq
    me_mid = lax.axis_index("mid")
    me_off = lax.axis_index("off")
    tr_dev = traces.shape[1]
    count = shrink_level.shape[0] // (n_mid * n_off)
    width = 2 * count
    pack = max(1, min(tr_dev, 128 // width))
    n_traces = total * tr_dev
    n_mids = n_traces // NOFF
    f32, bf16 = jnp.float32, jnp.bfloat16

    filtered = jnp.dot(traces[0], time_filter, preferred_element_type=f32).astype(bf16)
    spectra = jnp.dot(filtered, dft, preferred_element_type=f32).astype(bf16)
    blocks = spectra.reshape(pack, tr_dev // pack, total, width)
    blocks = jnp.transpose(blocks, (2, 1, 0, 3)).reshape(total, tr_dev // pack, pack * width)
    own_levels = lax.dynamic_slice_in_dim(shrink_level, (me_mid * n_off + me_off) * count, count)
    level = jnp.broadcast_to(own_levels[:, None, None], (count, 1, NP))
    own_ids = midpoint_of * NOFF + offset_of
    if n_traces <= 4096:
        own_ids = jnp.transpose(own_ids.reshape(total // n_off, pack, tr_dev // pack), (1, 0, 2)).reshape(pack, -1)
        returned = fused(blocks, own_ids, level, weights, sizes, pack)
    else:
        rows, ids = swap(blocks, sizes, 0, own_ids)
        rows = rows.reshape(total, tr_dev // pack, pack, width)
        rows = jnp.transpose(rows, (0, 2, 1, 3)).reshape(n_traces, width)
        cell_of = ids.reshape(n_traces)
        gather = jnp.zeros((n_traces, width), bf16).at[cell_of].set(rows)
        edged = jnp.pad(gather.reshape(n_mids, NOFF, 2, count).astype(f32), ((1, 1), (0, 0), (0, 0), (0, 0)))
        smooth = ((edged[:-2] + 2.0 * edged[1:-1] + edged[2:]) * 0.25).astype(bf16)
        smooth = jnp.transpose(smooth, (2, 3, 0, 1))
        mult = radon(smooth, level, weights, n_mid, n_off).reshape(width, n_traces)
        back = jnp.transpose(mult)[cell_of].reshape(total, pack, tr_dev // pack, width)
        back = jnp.transpose(back, (0, 2, 1, 3)).reshape(total, tr_dev // pack, pack * width)
        (returned,) = swap(back, sizes, 1)
    returned = returned.reshape(total, tr_dev // pack, pack, width)
    own_mult = jnp.transpose(returned, (2, 1, 0, 3)).reshape(tr_dev, total * width)
    clean = (spectra.astype(f32) - own_mult.astype(f32)).astype(bf16)
    sums = lax.dot_general(clean, dft, (((1,), (1,)), ((), ())), preferred_element_type=f32)
    return (2.0 * sums).astype(bf16)[None]


def solution(mesh):
    n_freq, n_mid, n_off = (mesh.shape[name] for name in ("freq", "mid", "off"))

    def run(traces, time_filter, midpoint_of, offset_of, shrink_level):
        n_freqs = shrink_level.shape[0]
        n_time = traces.shape[2]
        pieces = n_freq * n_mid * n_off
        dft = dft_table(n_time, pieces, n_freqs // pieces).reshape(n_time, n_freq, n_mid, n_off, -1)
        dft = np.ascontiguousarray(dft.transpose(0, 3, 2, 1, 4)).reshape(n_time, 2 * n_freqs)
        weights = radon_table(n_freqs)
        return jax.shard_map(
            on_device,
            mesh=mesh,
            in_specs=(
                P(),
                P(),
                P("off", ("group", "mid", "freq"), None),
                P(),
                P("off", "group"),
                P("off", "group"),
                P("freq"),
            ),
            out_specs=P("off", ("group", "mid", "freq"), None),
            check_vma=False,
        )(jnp.asarray(dft), jnp.asarray(weights), traces, time_filter, midpoint_of, offset_of, shrink_level)

    return run
```

```python
import functools
import math

import jax
import jax.numpy as jnp
import numpy as np
from jax import lax
from jax.experimental import pallas as pl
from jax.experimental.pallas import tpu as pltpu
from jax.sharding import PartitionSpec as P

NOFF = 128
NP = 128
radon_period = 4096
VMEM = pl.BlockSpec(memory_space=pltpu.VMEM)
ANY = pl.BlockSpec(memory_space=pl.ANY)


def dft_table(n_time, n_bands, band_size):
    sample = np.arange(n_time, dtype=np.int64)[:, None]
    freq_index = np.arange(n_bands * band_size, dtype=np.int64)[None, :]
    angle = 2.0 * np.pi * (sample * freq_index % n_time) / n_time
    scale_f = 1.0 / math.sqrt(n_time)
    cosine = (np.cos(angle) * scale_f).reshape(n_time, n_bands, band_size)
    sine = (-np.sin(angle) * scale_f).reshape(n_time, n_bands, band_size)
    table = np.stack([cosine, sine], axis=2).reshape(n_time, n_bands * 2 * band_size)
    return table.astype(np.float32).astype(jnp.bfloat16)


def radon_table(n_freqs):
    freq_index = np.arange(n_freqs, dtype=np.int64)[:, None, None]
    offset_index = np.arange(NOFF, dtype=np.int64)[None, :, None]
    slowness = np.arange(NP, dtype=np.int64)[None, None, :]
    turns = freq_index * slowness % radon_period * (offset_index * offset_index % radon_period) % radon_period
    circle = 2.0 * np.pi * np.arange(radon_period) / radon_period
    scale_r = 1.0 / math.sqrt(NOFF)
    cosine = (np.cos(circle) * scale_r).astype(np.float32).astype(jnp.bfloat16)[turns]
    sine = (np.sin(circle) * scale_r).astype(np.float32).astype(jnp.bfloat16)[turns]
    return np.stack([cosine, sine], axis=1).reshape(n_freqs, 2 * NOFF, NP)


def signal(barrier, **device):
    pl.semaphore_signal(barrier, inc=1, device_id=device, device_id_type=pl.DeviceIdType.MESH)


def send(src, dst, send_sem, recv_sem, **device):
    return pltpu.make_async_remote_copy(
        src_ref=src,
        dst_ref=dst,
        send_sem=send_sem,
        recv_sem=recv_sem,
        device_id=device,
        device_id_type=pl.DeviceIdType.MESH,
    )


def place(sizes):
    names = ("off", "mid", "freq")
    here = [lax.axis_index(name) for name in names]
    index = (here[0] * sizes[1] + here[1]) * sizes[2] + here[2]
    total = sizes[0] * sizes[1] * sizes[2]

    def ahead(i):
        there = (index + i) % total
        return there, dict(off=there // (sizes[1] * sizes[2]), mid=there // sizes[2] % sizes[1], freq=there % sizes[2])

    return index, total, ahead


def swap_kernel(sizes, with_ids, *refs):
    if with_ids:
        blocks, ids, got, got_ids, own_sem, send_sem, recv_sem, id_own, id_send, id_recv = refs
    else:
        blocks, got, own_sem, send_sem, recv_sem = refs
    index, total, ahead = place(sizes)
    n_off = sizes[0]
    barrier = pltpu.get_barrier_semaphore()

    @pl.loop(1, total)
    def _(i):
        signal(barrier, **ahead(i)[1])

    own = pltpu.make_async_copy(blocks.at[index], got.at[index], own_sem)
    own.start()
    pl.semaphore_wait(barrier, total - 1)

    def block_copy(i):
        there, device = ahead(i)
        return send(blocks.at[there], got.at[index], send_sem.at[i], recv_sem.at[i], **device)

    def id_copy(d):
        off = lax.axis_index("off")
        return send(ids, got_ids.at[off], id_send.at[d], id_recv.at[d], off=(off + d) % n_off)

    if with_ids:
        own_ids = pltpu.make_async_copy(ids, got_ids.at[lax.axis_index("off")], id_own)
        own_ids.start()
        for d in range(1, n_off):
            id_copy(d).start()

    @pl.loop(1, total)
    def _(i):
        block_copy(i).start()

    own.wait()
    if with_ids:
        own_ids.wait()
        for d in range(1, n_off):
            id_copy(d).wait()

    @pl.loop(1, total)
    def _(i):
        block_copy(i).wait()


def swap(blocks, sizes, collective_id, ids=None):
    total, n_off = blocks.shape[0], sizes[0]
    dma = pltpu.SemaphoreType.DMA
    shapes = [jax.ShapeDtypeStruct(blocks.shape, blocks.dtype)]
    scratch = [dma, dma((total,)), dma((total,))]
    operands = [blocks]
    if ids is not None:
        shapes.append(jax.ShapeDtypeStruct((n_off,) + ids.shape, ids.dtype))
        scratch += [dma, dma((n_off,)), dma((n_off,))]
        operands.append(ids)
    return pl.pallas_call(
        functools.partial(swap_kernel, sizes, ids is not None),
        out_shape=shapes,
        in_specs=[VMEM] * len(operands),
        out_specs=[VMEM] * len(shapes),
        scratch_shapes=scratch,
        compiler_params=pltpu.CompilerParams(collective_id=collective_id, has_side_effects=True),
    )(*operands)


def radon_kernel(n_mid, n_off, smooth, level, table, out, weights, sem):
    count, mids = smooth.shape[1:3]
    q = (lax.axis_index("freq") * n_mid + lax.axis_index("mid")) * n_off + lax.axis_index("off")
    fetch = pltpu.make_async_copy(table.at[pl.ds(q * count, count)], weights, sem)
    fetch.start()
    re = smooth[0].astype(jnp.float32)
    im = smooth[1].astype(jnp.float32)
    first = jnp.concatenate([re, -im], axis=2)
    second = jnp.concatenate([im, re], axis=2)
    x = jnp.concatenate([first, second], axis=1).astype(jnp.bfloat16)
    fetch.wait()
    model = lax.dot_general(x, weights[...], (((2,), (1,)), ((0,), (0,))), preferred_element_type=jnp.float32)
    model_re, model_im = model[:, :mids], model[:, mids:]
    power = model_re * model_re + model_im * model_im
    keep = (lax.broadcasted_iota(jnp.int32, power.shape, 2) >= NP // 4).astype(jnp.float32)
    lev = level[...]
    factor = power / (power + lev * lev) * keep
    kept = jnp.concatenate([model_re * factor, model_im * factor], axis=1).astype(jnp.bfloat16)
    both = lax.dot_general(kept, weights[...], (((2,), (2,)), ((0,), (0,))), preferred_element_type=jnp.float32)
    out[0] = (both[:, :mids, :NOFF] + both[:, mids:, NOFF:]).astype(jnp.bfloat16)
    out[1] = (both[:, mids:, :NOFF] - both[:, :mids, NOFF:]).astype(jnp.bfloat16)


def radon(smooth, level, table, n_mid, n_off):
    count = smooth.shape[1]
    return pl.pallas_call(
        functools.partial(radon_kernel, n_mid, n_off),
        out_shape=jax.ShapeDtypeStruct(smooth.shape, jnp.bfloat16),
        in_specs=[VMEM, VMEM, ANY],
        out_specs=VMEM,
        scratch_shapes=[pltpu.VMEM((count, 2 * NOFF, NP), jnp.bfloat16), pltpu.SemaphoreType.DMA],
        compiler_params=pltpu.CompilerParams(vmem_limit_bytes=24 * 1024 * 1024),
    )(smooth, level, table)


def fused_kernel(sizes, pack, traces, time_filter, ids, level, dft_hbm, table, out, dft, spec, blocks, ret, f_sem, got, got_ids, back, weights, near, same, cube, t_sem, own_sem, send_sem, recv_sem, id_own, id_send, id_recv):
    index, total, ahead = place(sizes)
    n_off, n_mid, n_freq = sizes
    off = lax.axis_index("off")
    f32, bf16 = jnp.float32, jnp.bfloat16
    width, mids = cube.shape[:2]
    count = width // 2
    n_cells = mids * NOFF
    per_half = ids.shape[1]
    barrier = pltpu.get_barrier_semaphore()

    @pl.loop(1, total)
    def _(i):
        signal(barrier, **ahead(i)[1])

    q = (lax.axis_index("freq") * n_mid + lax.axis_index("mid")) * n_off + off
    fetch = pltpu.make_async_copy(table.at[pl.ds(q * count, count)], weights, t_sem)
    fetch_dft = pltpu.make_async_copy(dft_hbm, dft, f_sem)
    fetch_dft.start()
    fetch.start()
    own_ids = pltpu.make_async_copy(ids, got_ids.at[off], id_own)
    own_ids.start()
    filtered = jnp.dot(traces[...], time_filter[...], preferred_element_type=f32).astype(bf16)
    fetch_dft.wait()
    spectra = jnp.dot(filtered, dft[...], preferred_element_type=f32).astype(bf16)
    spec[...] = spectra
    lines = blocks.shape[1]
    for d in range(total):
        parts = [spectra[pk * lines : (pk + 1) * lines, d * width : (d + 1) * width] for pk in range(pack)]
        blocks[d] = jnp.concatenate(parts, axis=1)
    own = pltpu.make_async_copy(blocks.at[index], got.at[index], own_sem.at[0])
    own.start()
    pl.semaphore_wait(barrier, total - 1)

    def block_copy(way, src, dst, i):
        there, device = ahead(i)
        return send(src.at[there], dst.at[index], send_sem.at[way, i], recv_sem.at[way, i], **device)

    def id_copy(d):
        return send(ids, got_ids.at[off], id_send.at[d], id_recv.at[d], off=(off + d) % n_off)

    for d in range(1, n_off):
        id_copy(d).start()

    @pl.loop(1, total)
    def _(i):
        block_copy(0, blocks, got, i).start()

    own_ids.wait()
    for d in range(1, n_off):
        id_copy(d).wait()
    step = 128

    @pl.loop(0, n_cells // step)
    def _(j):
        here = pl.multiple_of(j * step, step)
        cell = lax.broadcasted_iota(jnp.int32, (step, per_half), 0) + here
        for o in range(n_off):
            for pk in range(pack):
                away = jnp.abs(cell - got_ids[o, pl.ds(pk, 1), :])
                hit = jnp.where(away == 0, 1.0, 0.0)
                near[pk, o, pl.ds(here, step)] = (0.5 * hit + jnp.where(away == NOFF, 0.25, 0.0)).astype(bf16)
                same[pk, o, pl.ds(here, step)] = hit.astype(bf16)

    own.wait()

    @pl.loop(1, total)
    def _(i):
        block_copy(0, blocks, got, i).wait()

    rows = jnp.transpose(got[...].reshape(n_off * per_half, pack * width).astype(f32)).astype(bf16)
    smooth = jnp.zeros((width, n_cells), f32)
    for pk in range(pack):
        for o in range(n_off):
            smooth += lax.dot_general(
                rows[pk * width : (pk + 1) * width, o * per_half : (o + 1) * per_half],
                near[pk, o],
                (((1,), (1,)), ((), ())),
                preferred_element_type=f32,
            )
    for c in range(mids):
        cube[:, c, :] = smooth[:, c * NOFF : (c + 1) * NOFF]
    re, im = cube[pl.ds(0, count)], cube[pl.ds(count, count)]
    first = jnp.concatenate([re, -im], axis=2)
    second = jnp.concatenate([im, re], axis=2)
    x = jnp.concatenate([first, second], axis=1).astype(bf16)
    fetch.wait()
    model = lax.dot_general(x, weights[...], (((2,), (1,)), ((0,), (0,))), preferred_element_type=f32)
    model_re, model_im = model[:, :mids], model[:, mids:]
    power = model_re * model_re + model_im * model_im
    keep = (lax.broadcasted_iota(jnp.int32, power.shape, 2) >= NP // 4).astype(f32)
    own_level = level[lax.axis_index("mid") * n_off + off]
    lev = jnp.transpose(jnp.broadcast_to(own_level, (NP, count)))[:, None, :]
    factor = power / (power + lev * lev) * keep
    kept = jnp.concatenate([model_re * factor, model_im * factor], axis=1).astype(bf16)
    both = lax.dot_general(kept, weights[...], (((2,), (2,)), ((0,), (0,))), preferred_element_type=f32)
    cube[pl.ds(0, count)] = both[:, :mids, :NOFF] + both[:, mids:, NOFF:]
    cube[pl.ds(count, count)] = both[:, mids:, :NOFF] - both[:, :mids, NOFF:]
    mult = jnp.concatenate([cube[:, c, :] for c in range(mids)], axis=1).astype(bf16)
    for o in range(n_off):
        routed = [jnp.dot(mult, same[pk, o], preferred_element_type=f32) for pk in range(pack)]
        routed = jnp.transpose(jnp.concatenate(routed, axis=0)).astype(bf16)
        part = total // n_off
        back[pl.ds(o * part, part)] = routed.reshape((part,) + blocks.shape[1:])
    own_back = pltpu.make_async_copy(back.at[index], ret.at[index], own_sem.at[1])
    own_back.start()

    @pl.loop(1, total)
    def _(i):
        block_copy(1, back, ret, i).start()

    own_back.wait()

    @pl.loop(1, total)
    def _(i):
        block_copy(1, back, ret, i).wait()

    own_mult = jnp.concatenate(
        [
            jnp.concatenate([ret[d][:, pk * width : (pk + 1) * width] for d in range(total)], axis=1)
            for pk in range(pack)
        ],
        axis=0,
    )
    clean = (spec[...].astype(f32) - own_mult.astype(f32)).astype(bf16)
    sums = lax.dot_general(clean, dft[...], (((1,), (1,)), ((), ())), preferred_element_type=f32)
    out[...] = (2.0 * sums).astype(bf16)


def fused(traces, time_filter, ids, level, dft, table, sizes, pack):
    n_off = sizes[0]
    total = n_off * sizes[1] * sizes[2]
    count = level.shape[2]
    shape = (total, traces.shape[0] // pack, pack * 2 * count)
    per_half = ids.shape[1]
    n_cells = n_off * per_half * pack
    dma = pltpu.SemaphoreType.DMA
    bf16 = jnp.bfloat16
    return pl.pallas_call(
        functools.partial(fused_kernel, sizes, pack),
        out_shape=jax.ShapeDtypeStruct(traces.shape, traces.dtype),
        in_specs=[VMEM, VMEM, VMEM, VMEM, ANY, ANY],
        out_specs=VMEM,
        scratch_shapes=[
            pltpu.VMEM(dft.shape, bf16),
            pltpu.VMEM((traces.shape[0], dft.shape[1]), bf16),
            pltpu.VMEM(shape, bf16),
            pltpu.VMEM(shape, bf16),
            dma,
            pltpu.VMEM(shape, bf16),
            pltpu.VMEM((n_off,) + ids.shape, jnp.int32),
            pltpu.VMEM(shape, bf16),
            pltpu.VMEM((count, 2 * NOFF, NP), bf16),
            pltpu.VMEM((pack, n_off, n_cells, per_half), bf16),
            pltpu.VMEM((pack, n_off, n_cells, per_half), bf16),
            pltpu.VMEM((2 * count, n_cells // NOFF, NOFF), jnp.float32),
            dma,
            dma((2,)),
            dma((2, total)),
            dma((2, total)),
            dma,
            dma((n_off,)),
            dma((n_off,)),
        ],
        compiler_params=pltpu.CompilerParams(
            collective_id=2, has_side_effects=True, vmem_limit_bytes=40 * 1024 * 1024
        ),
    )(traces, time_filter, ids, level, dft, table)


def on_device(dft, weights, traces, time_filter, midpoint_of, offset_of, shrink_level):
    n_mid = lax.axis_size("mid")
    n_freq = lax.axis_size("freq")
    n_off = lax.axis_size("off")
    sizes = (n_off, n_mid, n_freq)
    total = n_off * n_mid * n_freq
    me_mid = lax.axis_index("mid")
    me_off = lax.axis_index("off")
    tr_dev = traces.shape[1]
    count = shrink_level.shape[0] // (n_mid * n_off)
    width = 2 * count
    pack = max(1, min(tr_dev, 128 // width))
    n_traces = total * tr_dev
    n_mids = n_traces // NOFF
    f32, bf16 = jnp.float32, jnp.bfloat16

    own_ids = midpoint_of * NOFF + offset_of
    if n_traces <= 4096:
        own_ids = jnp.transpose(own_ids.reshape(total // n_off, pack, tr_dev // pack), (1, 0, 2)).reshape(pack, -1)
        level = shrink_level.reshape(n_mid * n_off, 1, count)
        return fused(traces[0], time_filter, own_ids, level, dft, weights, sizes, pack)[None]
    filtered = jnp.dot(traces[0], time_filter, preferred_element_type=f32).astype(bf16)
    spectra = jnp.dot(filtered, dft, preferred_element_type=f32).astype(bf16)
    blocks = spectra.reshape(pack, tr_dev // pack, total, width)
    blocks = jnp.transpose(blocks, (2, 1, 0, 3)).reshape(total, tr_dev // pack, pack * width)
    own_levels = lax.dynamic_slice_in_dim(shrink_level, (me_mid * n_off + me_off) * count, count)
    level = jnp.broadcast_to(own_levels[:, None, None], (count, 1, NP))
    rows, ids = swap(blocks, sizes, 0, own_ids)
    rows = rows.reshape(total, tr_dev // pack, pack, width)
    rows = jnp.transpose(rows, (0, 2, 1, 3)).reshape(n_traces, width)
    cell_of = ids.reshape(n_traces)
    gather = jnp.zeros((n_traces, width), bf16).at[cell_of].set(rows)
    edged = jnp.pad(gather.reshape(n_mids, NOFF, 2, count).astype(f32), ((1, 1), (0, 0), (0, 0), (0, 0)))
    smooth = ((edged[:-2] + 2.0 * edged[1:-1] + edged[2:]) * 0.25).astype(bf16)
    smooth = jnp.transpose(smooth, (2, 3, 0, 1))
    mult = radon(smooth, level, weights, n_mid, n_off).reshape(width, n_traces)
    back = jnp.transpose(mult)[cell_of].reshape(total, pack, tr_dev // pack, width)
    back = jnp.transpose(back, (0, 2, 1, 3)).reshape(total, tr_dev // pack, pack * width)
    (returned,) = swap(back, sizes, 1)
    returned = returned.reshape(total, tr_dev // pack, pack, width)
    own_mult = jnp.transpose(returned, (2, 1, 0, 3)).reshape(tr_dev, total * width)
    clean = (spectra.astype(f32) - own_mult.astype(f32)).astype(bf16)
    sums = lax.dot_general(clean, dft, (((1,), (1,)), ((), ())), preferred_element_type=f32)
    return (2.0 * sums).astype(bf16)[None]


def solution(mesh):
    n_freq, n_mid, n_off = (mesh.shape[name] for name in ("freq", "mid", "off"))

    def run(traces, time_filter, midpoint_of, offset_of, shrink_level):
        n_freqs = shrink_level.shape[0]
        n_time = traces.shape[2]
        pieces = n_freq * n_mid * n_off
        dft = dft_table(n_time, pieces, n_freqs // pieces).reshape(n_time, n_freq, n_mid, n_off, -1)
        dft = np.ascontiguousarray(dft.transpose(0, 3, 2, 1, 4)).reshape(n_time, 2 * n_freqs)
        weights = radon_table(n_freqs)
        return jax.shard_map(
            on_device,
            mesh=mesh,
            in_specs=(
                P(),
                P(),
                P("off", ("group", "mid", "freq"), None),
                P(),
                P("off", "group"),
                P("off", "group"),
                P("freq"),
            ),
            out_specs=P("off", ("group", "mid", "freq"), None),
            check_vma=False,
        )(jnp.asarray(dft), jnp.asarray(weights), traces, time_filter, midpoint_of, offset_of, shrink_level)

    return run
```

```python
import functools
import math

import jax
import jax.numpy as jnp
import numpy as np
from jax import lax
from jax.experimental import pallas as pl
from jax.experimental.pallas import tpu as pltpu
from jax.sharding import PartitionSpec as P

NOFF = 128
NP = 128
radon_period = 4096
VMEM = pl.BlockSpec(memory_space=pltpu.VMEM)
ANY = pl.BlockSpec(memory_space=pl.ANY)


def dft_table(n_time, n_bands, band_size):
    sample = np.arange(n_time, dtype=np.int64)[:, None]
    freq_index = np.arange(n_bands * band_size, dtype=np.int64)[None, :]
    angle = 2.0 * np.pi * (sample * freq_index % n_time) / n_time
    scale_f = 1.0 / math.sqrt(n_time)
    cosine = (np.cos(angle) * scale_f).reshape(n_time, n_bands, band_size)
    sine = (-np.sin(angle) * scale_f).reshape(n_time, n_bands, band_size)
    table = np.stack([cosine, sine], axis=2).reshape(n_time, n_bands * 2 * band_size)
    return table.astype(np.float32).astype(jnp.bfloat16)


def radon_table(n_freqs):
    freq_index = np.arange(n_freqs, dtype=np.int64)[:, None, None]
    offset_index = np.arange(NOFF, dtype=np.int64)[None, :, None]
    slowness = np.arange(NP, dtype=np.int64)[None, None, :]
    turns = freq_index * slowness % radon_period * (offset_index * offset_index % radon_period) % radon_period
    circle = 2.0 * np.pi * np.arange(radon_period) / radon_period
    scale_r = 1.0 / math.sqrt(NOFF)
    cosine = (np.cos(circle) * scale_r).astype(np.float32).astype(jnp.bfloat16)[turns]
    sine = (np.sin(circle) * scale_r).astype(np.float32).astype(jnp.bfloat16)[turns]
    return np.stack([cosine, sine], axis=1).reshape(n_freqs, 2 * NOFF, NP)


def signal(barrier, **device):
    pl.semaphore_signal(barrier, inc=1, device_id=device, device_id_type=pl.DeviceIdType.MESH)


def send(src, dst, send_sem, recv_sem, **device):
    return pltpu.make_async_remote_copy(
        src_ref=src,
        dst_ref=dst,
        send_sem=send_sem,
        recv_sem=recv_sem,
        device_id=device,
        device_id_type=pl.DeviceIdType.MESH,
    )


def place(sizes):
    names = ("off", "mid", "freq")
    here = [lax.axis_index(name) for name in names]
    index = (here[0] * sizes[1] + here[1]) * sizes[2] + here[2]
    total = sizes[0] * sizes[1] * sizes[2]

    def ahead(i):
        there = (index + i) % total
        return there, dict(off=there // (sizes[1] * sizes[2]), mid=there // sizes[2] % sizes[1], freq=there % sizes[2])

    return index, total, ahead


def swap_kernel(sizes, with_ids, *refs):
    if with_ids:
        blocks, ids, got, got_ids, own_sem, send_sem, recv_sem, id_own, id_send, id_recv = refs
    else:
        blocks, got, own_sem, send_sem, recv_sem = refs
    index, total, ahead = place(sizes)
    n_off = sizes[0]
    barrier = pltpu.get_barrier_semaphore()

    @pl.loop(1, total)
    def _(i):
        signal(barrier, **ahead(i)[1])

    own = pltpu.make_async_copy(blocks.at[index], got.at[index], own_sem)
    own.start()
    pl.semaphore_wait(barrier, total - 1)

    def block_copy(i):
        there, device = ahead(i)
        return send(blocks.at[there], got.at[index], send_sem.at[i], recv_sem.at[i], **device)

    def id_copy(d):
        off = lax.axis_index("off")
        return send(ids, got_ids.at[off], id_send.at[d], id_recv.at[d], off=(off + d) % n_off)

    if with_ids:
        own_ids = pltpu.make_async_copy(ids, got_ids.at[lax.axis_index("off")], id_own)
        own_ids.start()
        for d in range(1, n_off):
            id_copy(d).start()

    @pl.loop(1, total)
    def _(i):
        block_copy(i).start()

    own.wait()
    if with_ids:
        own_ids.wait()
        for d in range(1, n_off):
            id_copy(d).wait()

    @pl.loop(1, total)
    def _(i):
        block_copy(i).wait()


def swap(blocks, sizes, collective_id, ids=None):
    total, n_off = blocks.shape[0], sizes[0]
    dma = pltpu.SemaphoreType.DMA
    shapes = [jax.ShapeDtypeStruct(blocks.shape, blocks.dtype)]
    scratch = [dma, dma((total,)), dma((total,))]
    operands = [blocks]
    if ids is not None:
        shapes.append(jax.ShapeDtypeStruct((n_off,) + ids.shape, ids.dtype))
        scratch += [dma, dma((n_off,)), dma((n_off,))]
        operands.append(ids)
    return pl.pallas_call(
        functools.partial(swap_kernel, sizes, ids is not None),
        out_shape=shapes,
        in_specs=[VMEM] * len(operands),
        out_specs=[VMEM] * len(shapes),
        scratch_shapes=scratch,
        compiler_params=pltpu.CompilerParams(collective_id=collective_id, has_side_effects=True),
    )(*operands)


def radon_kernel(n_mid, n_off, smooth, level, table, out, weights, sem):
    count, mids = smooth.shape[1:3]
    q = (lax.axis_index("freq") * n_mid + lax.axis_index("mid")) * n_off + lax.axis_index("off")
    fetch = pltpu.make_async_copy(table.at[pl.ds(q * count, count)], weights, sem)
    fetch.start()
    re = smooth[0].astype(jnp.float32)
    im = smooth[1].astype(jnp.float32)
    first = jnp.concatenate([re, -im], axis=2)
    second = jnp.concatenate([im, re], axis=2)
    x = jnp.concatenate([first, second], axis=1).astype(jnp.bfloat16)
    fetch.wait()
    model = lax.dot_general(x, weights[...], (((2,), (1,)), ((0,), (0,))), preferred_element_type=jnp.float32)
    model_re, model_im = model[:, :mids], model[:, mids:]
    power = model_re * model_re + model_im * model_im
    keep = (lax.broadcasted_iota(jnp.int32, power.shape, 2) >= NP // 4).astype(jnp.float32)
    lev = level[...]
    factor = power / (power + lev * lev) * keep
    kept = jnp.concatenate([model_re * factor, model_im * factor], axis=1).astype(jnp.bfloat16)
    both = lax.dot_general(kept, weights[...], (((2,), (2,)), ((0,), (0,))), preferred_element_type=jnp.float32)
    out[0] = (both[:, :mids, :NOFF] + both[:, mids:, NOFF:]).astype(jnp.bfloat16)
    out[1] = (both[:, mids:, :NOFF] - both[:, :mids, NOFF:]).astype(jnp.bfloat16)


def radon(smooth, level, table, n_mid, n_off):
    count = smooth.shape[1]
    return pl.pallas_call(
        functools.partial(radon_kernel, n_mid, n_off),
        out_shape=jax.ShapeDtypeStruct(smooth.shape, jnp.bfloat16),
        in_specs=[VMEM, VMEM, ANY],
        out_specs=VMEM,
        scratch_shapes=[pltpu.VMEM((count, 2 * NOFF, NP), jnp.bfloat16), pltpu.SemaphoreType.DMA],
        compiler_params=pltpu.CompilerParams(vmem_limit_bytes=24 * 1024 * 1024),
    )(smooth, level, table)


def fused_kernel(sizes, pack, traces, time_filter, ids, level, dft_hbm, table, out, dft, spec, blocks, ret, f_sem, got, got_ids, back, weights, near, same, cube, t_sem, own_sem, send_sem, recv_sem, id_own, id_send, id_recv):
    index, total, ahead = place(sizes)
    n_off, n_mid, n_freq = sizes
    off = lax.axis_index("off")
    f32, bf16 = jnp.float32, jnp.bfloat16
    width, mids = cube.shape[:2]
    count = width // 2
    n_cells = mids * NOFF
    per_half = ids.shape[1]
    barrier = pltpu.get_barrier_semaphore()

    @pl.loop(1, total)
    def _(i):
        signal(barrier, **ahead(i)[1])

    q = (lax.axis_index("freq") * n_mid + lax.axis_index("mid")) * n_off + off
    fetch = pltpu.make_async_copy(table.at[pl.ds(q * count, count)], weights, t_sem)
    fetch_dft = pltpu.make_async_copy(dft_hbm, dft, f_sem)
    fetch_dft.start()
    fetch.start()
    own_ids = pltpu.make_async_copy(ids, got_ids.at[off], id_own)
    own_ids.start()
    filtered = jnp.dot(traces[...], time_filter[...], preferred_element_type=f32).astype(bf16)
    fetch_dft.wait()
    spectra = jnp.dot(filtered, dft[...], preferred_element_type=f32).astype(bf16)
    spec[...] = spectra
    lines = blocks.shape[1]
    for d in range(total):
        parts = [spectra[pk * lines : (pk + 1) * lines, d * width : (d + 1) * width] for pk in range(pack)]
        blocks[d] = jnp.concatenate(parts, axis=1)
    own = pltpu.make_async_copy(blocks.at[index], got.at[index], own_sem.at[0])
    own.start()
    pl.semaphore_wait(barrier, total - 1)

    def block_copy(way, src, dst, i):
        there, device = ahead(i)
        return send(src.at[there], dst.at[index], send_sem.at[way, i], recv_sem.at[way, i], **device)

    def id_copy(d):
        return send(ids, got_ids.at[off], id_send.at[d], id_recv.at[d], off=(off + d) % n_off)

    for d in range(1, n_off):
        id_copy(d).start()

    @pl.loop(1, total)
    def _(i):
        block_copy(0, blocks, got, i).start()

    own_ids.wait()
    for d in range(1, n_off):
        id_copy(d).wait()
    step = 128

    @pl.loop(0, n_cells // step)
    def _(j):
        here = pl.multiple_of(j * step, step)
        cell = lax.broadcasted_iota(jnp.int32, (step, per_half), 0) + here
        for o in range(n_off):
            for pk in range(pack):
                away = jnp.abs(cell - got_ids[o, pl.ds(pk, 1), :])
                hit = jnp.where(away == 0, 1.0, 0.0)
                near[pk, o, pl.ds(here, step)] = (0.5 * hit + jnp.where(away == NOFF, 0.25, 0.0)).astype(bf16)
                same[pk, o, pl.ds(here, step)] = hit.astype(bf16)

    own.wait()

    @pl.loop(1, total)
    def _(i):
        block_copy(0, blocks, got, i).wait()

    rows = jnp.transpose(got[...].reshape(n_off * per_half, pack * width).astype(f32)).astype(bf16)
    smooth = jnp.zeros((width, n_cells), f32)
    for pk in range(pack):
        for o in range(n_off):
            smooth += lax.dot_general(
                rows[pk * width : (pk + 1) * width, o * per_half : (o + 1) * per_half],
                near[pk, o],
                (((1,), (1,)), ((), ())),
                preferred_element_type=f32,
            )
    for c in range(mids):
        cube[:, c, :] = smooth[:, c * NOFF : (c + 1) * NOFF]
    re, im = cube[pl.ds(0, count)], cube[pl.ds(count, count)]
    first = jnp.concatenate([re, -im], axis=2)
    second = jnp.concatenate([im, re], axis=2)
    x = jnp.concatenate([first, second], axis=1).astype(bf16)
    fetch.wait()
    model = lax.dot_general(x, weights[...], (((2,), (1,)), ((0,), (0,))), preferred_element_type=f32)
    model_re, model_im = model[:, :mids], model[:, mids:]
    power = model_re * model_re + model_im * model_im
    keep = (lax.broadcasted_iota(jnp.int32, power.shape, 2) >= NP // 4).astype(f32)
    own_level = level[lax.axis_index("mid") * n_off + off]
    lev = jnp.transpose(jnp.broadcast_to(own_level, (NP, count)))[:, None, :]
    factor = power / (power + lev * lev) * keep
    kept = jnp.concatenate([model_re * factor, model_im * factor], axis=1).astype(bf16)
    both = lax.dot_general(kept, weights[...], (((2,), (2,)), ((0,), (0,))), preferred_element_type=f32)
    cube[pl.ds(0, count)] = both[:, :mids, :NOFF] + both[:, mids:, NOFF:]
    cube[pl.ds(count, count)] = both[:, mids:, :NOFF] - both[:, :mids, NOFF:]
    mult = jnp.concatenate([cube[:, c, :] for c in range(mids)], axis=1).astype(bf16)
    for o in range(n_off):
        routed = [jnp.dot(mult, same[pk, o], preferred_element_type=f32) for pk in range(pack)]
        routed = jnp.transpose(jnp.concatenate(routed, axis=0)).astype(bf16)
        part = total // n_off
        back[pl.ds(o * part, part)] = routed.reshape((part,) + blocks.shape[1:])
    own_back = pltpu.make_async_copy(back.at[index], ret.at[index], own_sem.at[1])
    own_back.start()

    @pl.loop(1, total)
    def _(i):
        block_copy(1, back, ret, i).start()

    own_back.wait()

    @pl.loop(1, total)
    def _(i):
        block_copy(1, back, ret, i).wait()

    own_mult = jnp.concatenate(
        [
            jnp.concatenate([ret[d][:, pk * width : (pk + 1) * width] for d in range(total)], axis=1)
            for pk in range(pack)
        ],
        axis=0,
    )
    clean = (spec[...].astype(f32) - own_mult.astype(f32)).astype(bf16)
    sums = lax.dot_general(clean, dft[...], (((1,), (1,)), ((), ())), preferred_element_type=f32)
    out[...] = (2.0 * sums).astype(bf16)


def fused(traces, time_filter, ids, level, dft, table, sizes, pack):
    n_off = sizes[0]
    total = n_off * sizes[1] * sizes[2]
    count = level.shape[2]
    shape = (total, traces.shape[0] // pack, pack * 2 * count)
    per_half = ids.shape[1]
    n_cells = n_off * per_half * pack
    dma = pltpu.SemaphoreType.DMA
    bf16 = jnp.bfloat16
    return pl.pallas_call(
        functools.partial(fused_kernel, sizes, pack),
        out_shape=jax.ShapeDtypeStruct(traces.shape, traces.dtype),
        in_specs=[VMEM, VMEM, VMEM, VMEM, ANY, ANY],
        out_specs=VMEM,
        scratch_shapes=[
            pltpu.VMEM(dft.shape, bf16),
            pltpu.VMEM((traces.shape[0], dft.shape[1]), bf16),
            pltpu.VMEM(shape, bf16),
            pltpu.VMEM(shape, bf16),
            dma,
            pltpu.VMEM(shape, bf16),
            pltpu.VMEM((n_off,) + ids.shape, jnp.int32),
            pltpu.VMEM(shape, bf16),
            pltpu.VMEM((count, 2 * NOFF, NP), bf16),
            pltpu.VMEM((pack, n_off, n_cells, per_half), bf16),
            pltpu.VMEM((pack, n_off, n_cells, per_half), bf16),
            pltpu.VMEM((2 * count, n_cells // NOFF, NOFF), jnp.float32),
            dma,
            dma((2,)),
            dma((2, total)),
            dma((2, total)),
            dma,
            dma((n_off,)),
            dma((n_off,)),
        ],
        compiler_params=pltpu.CompilerParams(
            collective_id=2, has_side_effects=True, vmem_limit_bytes=60 * 1024 * 1024
        ),
    )(traces, time_filter, ids, level, dft, table)


def on_device(dft, weights, traces, time_filter, midpoint_of, offset_of, shrink_level):
    n_mid = lax.axis_size("mid")
    n_freq = lax.axis_size("freq")
    n_off = lax.axis_size("off")
    sizes = (n_off, n_mid, n_freq)
    total = n_off * n_mid * n_freq
    me_mid = lax.axis_index("mid")
    me_off = lax.axis_index("off")
    tr_dev = traces.shape[1]
    count = shrink_level.shape[0] // (n_mid * n_off)
    width = 2 * count
    pack = max(1, min(tr_dev, 128 // width))
    n_traces = total * tr_dev
    n_mids = n_traces // NOFF
    f32, bf16 = jnp.float32, jnp.bfloat16

    own_ids = midpoint_of * NOFF + offset_of
    if n_traces <= 4096:
        own_ids = jnp.transpose(own_ids.reshape(total // n_off, pack, tr_dev // pack), (1, 0, 2)).reshape(pack, -1)
        level = shrink_level.reshape(n_mid * n_off, 1, count)
        return fused(traces[0], time_filter, own_ids, level, dft, weights, sizes, pack)[None]
    filtered = jnp.dot(traces[0], time_filter, preferred_element_type=f32).astype(bf16)
    spectra = jnp.dot(filtered, dft, preferred_element_type=f32).astype(bf16)
    blocks = spectra.reshape(pack, tr_dev // pack, total, width)
    blocks = jnp.transpose(blocks, (2, 1, 0, 3)).reshape(total, tr_dev // pack, pack * width)
    own_levels = lax.dynamic_slice_in_dim(shrink_level, (me_mid * n_off + me_off) * count, count)
    level = jnp.broadcast_to(own_levels[:, None, None], (count, 1, NP))
    rows, ids = swap(blocks, sizes, 0, own_ids)
    rows = rows.reshape(total, tr_dev // pack, pack, width)
    rows = jnp.transpose(rows, (0, 2, 1, 3)).reshape(n_traces, width)
    cell_of = ids.reshape(n_traces)
    gather = jnp.zeros((n_traces, width), bf16).at[cell_of].set(rows)
    edged = jnp.pad(gather.reshape(n_mids, NOFF, 2, count).astype(f32), ((1, 1), (0, 0), (0, 0), (0, 0)))
    smooth = ((edged[:-2] + 2.0 * edged[1:-1] + edged[2:]) * 0.25).astype(bf16)
    smooth = jnp.transpose(smooth, (2, 3, 0, 1))
    mult = radon(smooth, level, weights, n_mid, n_off).reshape(width, n_traces)
    back = jnp.transpose(mult)[cell_of].reshape(total, pack, tr_dev // pack, width)
    back = jnp.transpose(back, (0, 2, 1, 3)).reshape(total, tr_dev // pack, pack * width)
    (returned,) = swap(back, sizes, 1)
    returned = returned.reshape(total, tr_dev // pack, pack, width)
    own_mult = jnp.transpose(returned, (2, 1, 0, 3)).reshape(tr_dev, total * width)
    clean = (spectra.astype(f32) - own_mult.astype(f32)).astype(bf16)
    sums = lax.dot_general(clean, dft, (((1,), (1,)), ((), ())), preferred_element_type=f32)
    return (2.0 * sums).astype(bf16)[None]


def solution(mesh):
    n_freq, n_mid, n_off = (mesh.shape[name] for name in ("freq", "mid", "off"))

    def run(traces, time_filter, midpoint_of, offset_of, shrink_level):
        n_freqs = shrink_level.shape[0]
        n_time = traces.shape[2]
        pieces = n_freq * n_mid * n_off
        dft = dft_table(n_time, pieces, n_freqs // pieces).reshape(n_time, n_freq, n_mid, n_off, -1)
        dft = np.ascontiguousarray(dft.transpose(0, 3, 2, 1, 4)).reshape(n_time, 2 * n_freqs)
        weights = radon_table(n_freqs)
        return jax.shard_map(
            on_device,
            mesh=mesh,
            in_specs=(
                P(),
                P(),
                P("off", ("group", "mid", "freq"), None),
                P(),
                P("off", "group"),
                P("off", "group"),
                P("freq"),
            ),
            out_specs=P("off", ("group", "mid", "freq"), None),
            check_vma=False,
        )(jnp.asarray(dft), jnp.asarray(weights), traces, time_filter, midpoint_of, offset_of, shrink_level)

    return run
```
